256 devices in a mesh: src: 16 (over y, x), tgt: 16 (over z, core).
Axes of the slice: x: 4, y: 4, z: 8, core: 2. Of those that a mesh axis runs over, the one named last changes fastest.
Arguments:
- pcs_source: bfloat16 [30, 32768], P(None, 'src'), may hold values from -6 to 10
- pcs_target: bfloat16 [30, 32768], P(None, 'tgt'), may hold values from -6 to 6
- growth: float32 [32768], P('src'), may hold values from 0.25 to 4
- scores: bfloat16 [32768, 128], P('src'), may hold values from -6 to 6
Outputs:
- source_potential: float32 [32768], P('src')
- target_potential: float32 [32768], P('tgt')
- transported: float32 [32768, 128], P('tgt')
The draws below stay inside these ranges and needn't reach their ends.
All inputs are finite; a program needn't handle non-finite values.
Results may differ from the reference program's by a relative error of at most 0.0029.
Values sent between devices are 32-bit elements; how exact they have to be, the bound alone decides.
No kernel may reach another device: no remote copies, remote signals or barrier semaphores. Data moves between devices by JAX's collectives and lax.ppermute only.
A program may use at most 64 MiB of HBM per device.

```python
import math
import jax
import jax.numpy as jnp
from jax import lax

PCS = 30
PROG = 128
ITERS = 2
NS = 32768
NT = 32768


def draw_pcs_source(key, part):
    base = jnp.clip(jax.random.normal(key, (PCS, NS), jnp.float32), -6.0, 6.0)
    return base.astype(jnp.bfloat16)


def shard_levels(key, dims, cuts, low, top_value):
    def one(dim, shards_of):
        draws = jax.random.uniform(jax.random.fold_in(jax.random.fold_in(key, 6), dim), (shards_of,), jnp.float32, low / len(cuts), top_value / len(cuts))
        return jnp.repeat(jnp.exp(draws), dims[dim] // shards_of).reshape((-1,) + (1,) * (len(dims) - dim - 1))

    level = one(*cuts[0])
    for cut in cuts[1:]:
        level = level * one(*cut)
    return level


def scatter_about(key, dims, deviation, limit, cuts=(), held_as=jnp.bfloat16):
    values = jax.random.normal(key, dims, jnp.float32) * deviation
    if len(cuts) > 0:
        values = shard_levels(key, dims, cuts, -0.22, 0.18) * values
    return jnp.clip(values, min=-limit, max=limit).astype(held_as)


def setup_inputs(seed: int = 0) -> dict:
    arg_keys = jax.random.split(jax.random.key(seed), 5)
    return {
        "pcs_source": draw_pcs_source(jax.random.fold_in(arg_keys[4], 71), 0),
        "pcs_target": scatter_about(arg_keys[1], (PCS, NT), 1.0, 6.0, ((1, 16),)),
        "growth": jnp.clip(jnp.exp(math.log(4.0) - 2.7725887 * jax.random.uniform(arg_keys[2], (NS,), jnp.float32) ** shard_levels(arg_keys[2], (NS,), ((0, 16),), -0.2, 0.2)), 0.25, 4.0),
        "scores": scatter_about(arg_keys[3], (NS, PROG), 1.0, 6.0, ((0, 16),)),
    }


EPSILON = 0.05
MARGIN = 1.0
FACTOR = MARGIN / (MARGIN + EPSILON)


def cost_tile(left, right):
    cross = lax.dot_general(left, right, (((0,), (0,)), ((), ())), preferred_element_type=jnp.float32)
    left_wide = left.astype(jnp.float32)
    right_wide = right.astype(jnp.float32)
    left_sq = jnp.sum(left_wide * left_wide, axis=0)
    right_sq = jnp.sum(right_wide * right_wide, axis=0)
    return (left_sq[:, None] + right_sq[None, :] - 2.0 * cross) / left.shape[0]


def stacked(coords, width):
    return jnp.transpose(coords.reshape(coords.shape[0], -1, width), (1, 0, 2))


def log_sum_rows(logits):
    peak = jnp.max(logits, axis=1)
    return peak + jnp.log(jnp.sum(jnp.exp(logits - peak[:, None]), axis=1))


def reference(pcs_source, pcs_target, growth, scores):
    total_sources = pcs_source.shape[1]
    total_targets = pcs_target.shape[1]
    source_width = math.gcd(total_sources, 256)
    target_width = math.gcd(total_targets, 256)
    source_blocks = stacked(pcs_source, source_width)
    target_blocks = stacked(pcs_target, target_width)
    log_a = jnp.log(growth) - jnp.log(jnp.float32(total_sources))
    log_b = -jnp.log(jnp.float32(total_targets))
    source_potential = jnp.zeros((total_sources,), jnp.float32)
    target_potential = jnp.zeros((total_targets,), jnp.float32)
    for step in range(ITERS):
        gpot = target_potential
        rows = lax.map(lambda block: log_sum_rows((gpot[None, :] - cost_tile(block, pcs_target)) / EPSILON), source_blocks).reshape(-1)
        source_potential = FACTOR * (EPSILON * log_a - EPSILON * rows)
        fpot = source_potential
        columns = lax.map(lambda block: log_sum_rows((fpot[None, :] - cost_tile(block, pcs_source)) / EPSILON), target_blocks).reshape(-1)
        target_potential = FACTOR * (EPSILON * log_b - EPSILON * columns)

    def carry_block(pair):
        block, gblock = pair
        tile = cost_tile(block, pcs_source)
        plan = jnp.exp((source_potential[None, :] + gblock[:, None] - tile) / EPSILON)
        mass = jnp.sum(plan, axis=1)
        carried = jnp.dot(plan.astype(jnp.bfloat16), scores, preferred_element_type=jnp.float32)
        return carried / mass[:, None]

    transported = lax.map(carry_block, (target_blocks, target_potential.reshape(-1, target_width))).reshape(total_targets, -1)
    return source_potential, target_potential, transported
```

```python
import functools
import math

import jax
import jax.numpy as jnp
from jax import lax
from jax.experimental import pallas as pl
from jax.experimental.pallas import tpu as pltpu
from jax.sharding import PartitionSpec as P

ITERS = 2
EPSILON = 0.05
MARGIN = 1.0
FACTOR = MARGIN / (MARGIN + EPSILON)

UNIT = EPSILON * math.log(2.0)
LOW, HIGH = 2.0**-90, 2.0**100
STATIC, DEPTH = 96, 112
TILE = 256
f32, bf16 = jnp.float32, jnp.bfloat16


def split3(v):
    high = v.astype(bf16).astype(f32)
    rest = v - high
    mid = rest.astype(bf16).astype(f32)
    return high, mid, (rest - mid).astype(bf16).astype(f32)


def rows_of(values, count):
    row = lax.broadcasted_iota(jnp.int32, (count, values[0].shape[-1]), 0)
    out = jnp.zeros(row.shape, f32)
    for k, v in enumerate(values):
        out = jnp.where(row == k, v, out)
    return out.astype(bf16)


def set_source(left, u):
    one = jnp.ones_like(u)
    left[STATIC:, :] = rows_of([*split3(u), one, one, one], DEPTH - STATIC)


def set_target(right, v):
    one = jnp.ones_like(v)
    right[STATIC:, :] = rows_of([one, one, one, *split3(v)], DEPTH - STATIC)


def tile_of(ref, k):
    return ref[:, pl.ds(pl.multiple_of(k * TILE, TILE), TILE)]


def logits(first, second):
    return lax.dot_general(first, second, (((0,), (0,)), ((), ())), preferred_element_type=f32)


def log_sum(first, second):
    count = first.shape[1] // TILE

    def peaks(k, peak):
        return jnp.maximum(peak, jnp.max(logits(tile_of(first, k), second[...]), axis=0, keepdims=True))

    peak = lax.fori_loop(0, count, peaks, jnp.full((1, second.shape[1]), -jnp.inf, f32))

    def totals(k, total):
        part = jnp.exp2(logits(tile_of(first, k), second[...]) - peak)
        return total + jnp.sum(part, axis=0, keepdims=True)

    total = lax.fori_loop(0, count, totals, jnp.zeros_like(peak))
    return peak, total


def merged(parts):
    peak = jnp.max(parts, axis=0)
    return peak + jnp.log2(jnp.sum(jnp.exp2(parts - peak[None]), axis=0))


def in_range(total):
    return jnp.logical_and(jnp.min(total) >= LOW, jnp.max(total) <= HIGH)


def send_copies(out, value):
    out[...] = jnp.broadcast_to(value[None], out.shape)


def weighted(weight, kernel):
    parts = lax.dot_general(
        rows_of(split3(weight), 16), kernel[...], (((1,), (1,)), ((), ())), preferred_element_type=f32
    )
    return jnp.sum(parts[:3], axis=0, keepdims=True)


def first_rows(scale, x_ref, y_ref, s_ref, out, left, right, asq, bsq, shift, kernel, sT, across):
    x = x_ref[...]
    y = y_ref[...].astype(f32)
    xw = x.astype(f32)
    pad = jnp.zeros((32 - x.shape[0], x.shape[1]), f32)
    xp = jnp.concatenate([xw, pad], axis=0).astype(bf16)
    for k, part in enumerate(split3(jnp.concatenate([y * (2.0 * scale), pad], axis=0))):
        left[32 * k : 32 * k + 32, :] = xp
        right[32 * k : 32 * k + 32, :] = part.astype(bf16)
    asq[...] = jnp.sum(xw * xw, axis=0, keepdims=True) * scale
    bsq[...] = jnp.sum(y * y, axis=0, keepdims=True) * scale
    set_source(left, -asq[...])
    set_target(right, -bsq[...])
    across[...] = jnp.transpose(right[...])
    size = x.shape[1]
    chunk = 512
    for n in range(0, size, chunk):
        part = jnp.dot(across[:TILE, :], left[:, n : n + chunk], preferred_element_type=f32)
        shift[:, n : n + chunk] = jnp.max(part, axis=0, keepdims=True)
    set_source(left, -asq[...] - shift[...])
    sums = []
    for n in range(0, size, chunk):
        total = jnp.zeros((8, chunk), f32)
        for k in range(0, size, TILE):
            part = jnp.dot(across[k : k + TILE, :], left[:, n : n + chunk], preferred_element_type=f32)
            part = jnp.exp2(part)
            kernel[k : k + TILE, n : n + chunk] = part.astype(bf16)
            total = total + jnp.sum(part.reshape(TILE // 8, 8, chunk), axis=0)
        sums.append(jnp.sum(total, axis=0, keepdims=True))
    total = jnp.concatenate(sums, axis=1)
    send_copies(out, shift[...] + jnp.log2(total))

    @pl.when(jnp.logical_not(in_range(total)))
    def _():
        set_source(left, -asq[...])
        peak, exact = log_sum(right, left)
        send_copies(out, peak + jnp.log2(exact))

    sT[...] = jnp.transpose(s_ref[...])


def source_weights(log_total, parts, growth, shift):
    rows = merged(parts[...])
    potential = FACTOR * (jnp.log2(growth[...]) - log_total - rows)
    log_weight = potential + shift[...]
    top = jnp.max(log_weight)
    return potential, jnp.exp2(log_weight - top), top


def columns(log_total, parts, growth, shift, kernel, left0, right0, asq, bsq, out, left, right):
    potential, weight, top = source_weights(log_total, parts, growth, shift)
    total = weighted(weight, kernel)
    send_copies(out, top + jnp.log2(total))

    @pl.when(jnp.logical_not(in_range(total)))
    def _():
        left[...] = left0[...]
        right[...] = right0[...]
        set_source(left, potential - asq[...])
        set_target(right, -bsq[...])
        peak, exact = log_sum(left, right)
        send_copies(out, peak + jnp.log2(exact))


def rows(log_total, parts, shift, kernel, left0, right0, asq, bsq, out, left, right):
    potential = FACTOR * (-log_total - merged(parts[...]))
    top = jnp.max(potential)
    weight = jnp.exp2(potential - top)
    parts3 = jnp.dot(rows_of(split3(weight), 16), kernel[...], preferred_element_type=f32)
    total = jnp.sum(parts3[:3], axis=0, keepdims=True)
    send_copies(out, shift[...] + top + jnp.log2(total))

    @pl.when(jnp.logical_not(in_range(total)))
    def _():
        left[...] = left0[...]
        right[...] = right0[...]
        set_source(left, -asq[...])
        set_target(right, potential - bsq[...])
        peak, exact = log_sum(right, left)
        send_copies(out, peak + jnp.log2(exact))


def put_blocks(out, carried, total, peak):
    count, lanes = out.shape[0], out.shape[2]
    progs = carried.shape[0]
    row = lax.broadcasted_iota(jnp.int32, (8, lanes), 0)
    for d in range(count):
        at = slice(d * lanes, (d + 1) * lanes)
        out[d, :progs, :] = carried[:, at]
        extra = jnp.where(row == 0, total[:, at], jnp.where(row == 1, peak[:, at], 0.0))
        out[d, progs:, :] = extra


def carry(log_total, parts, growth, shift, kernel, sT, left0, right0, asq, bsq, fout, out, left, right):
    potential, weight, top = source_weights(log_total, parts, growth, shift)
    fout[...] = potential * UNIT
    total = weighted(weight, kernel)
    scaled = (sT[...].astype(f32) * weight).astype(bf16)
    carried = lax.dot_general(
        scaled, kernel[...], (((1,), (1,)), ((), ())), preferred_element_type=f32
    )
    put_blocks(out, carried, total, jnp.full(total.shape, top, f32))

    @pl.when(jnp.logical_not(in_range(total)))
    def _():
        left[...] = left0[...]
        right[...] = right0[...]
        set_source(left, potential - asq[...])
        set_target(right, -bsq[...])
        peak, exact = log_sum(left, right)

        def step(k, sums):
            plan = jnp.exp2(logits(tile_of(left, k), right[...]) - peak).astype(bf16)
            return sums + jnp.dot(tile_of(sT, k), plan, preferred_element_type=f32)

        sums = lax.fori_loop(0, left.shape[1] // TILE, step, jnp.zeros(carried.shape, f32))
        put_blocks(out, sums, exact, peak)


def finish(log_total, parts, out):
    count, lanes = parts.shape[0], parts.shape[2]
    progs = parts.shape[1] - 8
    peaks = [parts[d, progs + 1 : progs + 2, :] for d in range(count)]
    peak = functools.reduce(jnp.maximum, peaks)
    total = jnp.zeros((1, lanes), f32)
    carried = jnp.zeros((progs, lanes), f32)
    for d in range(count):
        weight = jnp.exp2(peaks[d] - peak)
        total = total + weight * parts[d, progs : progs + 1, :]
        carried = carried + weight * parts[d, :progs, :]
    potential = FACTOR * (-log_total - peak - jnp.log2(total)) * UNIT
    block = jnp.transpose(carried / total)
    extra = jnp.broadcast_to(potential, (8, lanes))
    for d in range(count):
        out[d, :lanes, :] = block
        out[d, lanes:, :] = extra


def call(kernel, outs, scratch=(), flops=10**7, name=None):
    return pl.pallas_call(
        kernel,
        out_shape=outs,
        scratch_shapes=list(scratch),
        compiler_params=pltpu.CompilerParams(vmem_limit_bytes=40 << 20),
        cost_estimate=pl.CostEstimate(flops=flops, bytes_accessed=1 << 20, transcendentals=0),
        name=name,
    )


def exchanged(x, axis):
    return lax.all_to_all(x, axis, 0, 0, tiled=True)


def shards(pcs_source, pcs_target, growth, scores):
    count, size = pcs_source.shape
    progs = scores.shape[1]
    sources, targets = lax.axis_size("src"), lax.axis_size("tgt")
    log_sources = math.log2(size * sources)
    log_targets = math.log2(pcs_target.shape[1] * targets)
    scale = math.log2(math.e) / (EPSILON * count)
    shape = jax.ShapeDtypeStruct
    line = shape((1, size), f32)
    operand = shape((DEPTH, size), bf16)
    operands = [pltpu.VMEM((DEPTH, size), bf16), pltpu.VMEM((DEPTH, size), bf16)]
    to_targets, to_sources = shape((targets, 1, size), f32), shape((sources, 1, size), f32)
    growth = growth.reshape(1, size)

    local, left, right, asq, bsq, shift, kernel, sT = call(
        functools.partial(first_rows, scale),
        (to_targets, operand, operand, line, line, line, shape((size, size), bf16), shape((progs, size), bf16)),
        [pltpu.VMEM((size, DEPTH), bf16)],
        name="first_rows",
    )(pcs_source, pcs_target, scores)
    parts = exchanged(local, "tgt")
    fixed = (left, right, asq, bsq)
    for _ in range(ITERS - 1):
        local = call(functools.partial(columns, log_sources), to_sources, operands, name="columns")(
            parts, growth, shift, kernel, *fixed
        )
        parts = exchanged(local, "src")
        local = call(functools.partial(rows, log_targets), to_targets, operands, name="rows")(
            parts, shift, kernel, *fixed
        )
        parts = exchanged(local, "tgt")
    own = size // sources
    potential, blocks = call(
        functools.partial(carry, log_sources),
        (line, shape((sources, progs + 8, own), f32)),
        operands,
        name="carry",
    )(parts, growth, shift, kernel, sT, *fixed)
    blocks = exchanged(blocks, "src")
    result = call(functools.partial(finish, log_targets), shape((sources, own + 8, progs), f32), name="finish")(blocks)
    result = exchanged(result, "src")
    transported = result[:, :own].reshape(size, progs)
    return potential.reshape(size), result[:, own].reshape(size), transported


def solution(mesh):
    in_specs = (P(None, "src"), P(None, "tgt"), P("src"), P("src", None))
    out_specs = (P("src"), P("tgt"), P("tgt", None))
    return jax.shard_map(shards, mesh=mesh, in_specs=in_specs, out_specs=out_specs, check_vma=False)
```

```python
import functools
import math

import jax
import jax.numpy as jnp
from jax import lax
from jax.experimental import pallas as pl
from jax.experimental.pallas import tpu as pltpu
from jax.sharding import PartitionSpec as P

ITERS = 2
EPSILON = 0.05
MARGIN = 1.0
FACTOR = MARGIN / (MARGIN + EPSILON)

UNIT = EPSILON * math.log(2.0)
LOW, HIGH = 2.0**-90, 2.0**100
STATIC, DEPTH = 96, 112
TILE = 256
f32, bf16 = jnp.float32, jnp.bfloat16


def split3(v):
    high = v.astype(bf16).astype(f32)
    rest = v - high
    mid = rest.astype(bf16).astype(f32)
    return high, mid, (rest - mid).astype(bf16).astype(f32)


def rows_of(values, count):
    row = lax.broadcasted_iota(jnp.int32, (count, values[0].shape[-1]), 0)
    out = jnp.zeros(row.shape, f32)
    for k, v in enumerate(values):
        out = jnp.where(row == k, v, out)
    return out.astype(bf16)


def set_source(left, u):
    one = jnp.ones_like(u)
    left[STATIC:, :] = rows_of([*split3(u), one, one, one], DEPTH - STATIC)


def set_target(right, v):
    one = jnp.ones_like(v)
    right[STATIC:, :] = rows_of([one, one, one, *split3(v)], DEPTH - STATIC)


def tile_of(ref, k):
    return ref[:, pl.ds(pl.multiple_of(k * TILE, TILE), TILE)]


def logits(first, second):
    return lax.dot_general(first, second, (((0,), (0,)), ((), ())), preferred_element_type=f32)


def log_sum(first, second):
    count = first.shape[1] // TILE

    def peaks(k, peak):
        return jnp.maximum(peak, jnp.max(logits(tile_of(first, k), second[...]), axis=0, keepdims=True))

    peak = lax.fori_loop(0, count, peaks, jnp.full((1, second.shape[1]), -jnp.inf, f32))

    def totals(k, total):
        part = jnp.exp2(logits(tile_of(first, k), second[...]) - peak)
        return total + jnp.sum(part, axis=0, keepdims=True)

    total = lax.fori_loop(0, count, totals, jnp.zeros_like(peak))
    return peak, total


def merged(parts):
    peak = jnp.max(parts, axis=0)
    return peak + jnp.log2(jnp.sum(jnp.exp2(parts - peak[None]), axis=0))


def in_range(total):
    return jnp.logical_and(jnp.min(total) >= LOW, jnp.max(total) <= HIGH)


def send_copies(out, value):
    out[...] = jnp.broadcast_to(value[None], out.shape)


def first_rows(
    scale, x_ref, y_ref, out, left, right, asq, bsq, shift, kernel, turned
):
    x = x_ref[...]
    y = y_ref[...].astype(f32)
    xw = x.astype(f32)
    pad = jnp.zeros((32 - x.shape[0], x.shape[1]), f32)
    xp = jnp.concatenate([xw, pad], axis=0).astype(bf16)
    for k, part in enumerate(split3(jnp.concatenate([y * (2.0 * scale), pad], axis=0))):
        left[32 * k : 32 * k + 32, :] = xp
        right[32 * k : 32 * k + 32, :] = part.astype(bf16)
    asq[...] = jnp.sum(xw * xw, axis=0, keepdims=True) * scale
    bsq[...] = jnp.sum(y * y, axis=0, keepdims=True) * scale
    set_source(left, -asq[...])
    set_target(right, -bsq[...])
    turned[...] = jnp.transpose(right[...])
    size = x.shape[1]
    chunk = 512
    for n in range(0, size, chunk):
        part = jnp.dot(turned[:TILE, :], left[:, n : n + chunk], preferred_element_type=f32)
        shift[:, n : n + chunk] = jnp.max(part, axis=0, keepdims=True)
    set_source(left, -asq[...] - shift[...])
    sums = []
    for n in range(0, size, chunk):
        total = jnp.zeros((8, chunk), f32)
        for k in range(0, size, TILE):
            part = jnp.dot(turned[k : k + TILE, :], left[:, n : n + chunk], preferred_element_type=f32)
            part = jnp.exp2(part)
            kernel[k : k + TILE, n : n + chunk] = part.astype(bf16)
            total = total + jnp.sum(part.reshape(TILE // 8, 8, chunk), axis=0)
        sums.append(jnp.sum(total, axis=0, keepdims=True))
    total = jnp.concatenate(sums, axis=1)
    send_copies(out, shift[...] + jnp.log2(total))

    @pl.when(jnp.logical_not(in_range(total)))
    def _():
        set_source(left, -asq[...])
        peak, exact = log_sum(right, left)
        send_copies(out, peak + jnp.log2(exact))


def source_weights(log_total, parts, growth, shift):
    rows = merged(parts[...])
    potential = FACTOR * (jnp.log2(growth[...]) - log_total - rows)
    log_weight = potential + shift[...]
    top = jnp.max(log_weight)
    return potential, jnp.exp2(log_weight - top), top


def over_targets(weight, kernel):
    parts = jnp.dot(rows_of(split3(weight), 16), kernel[...], preferred_element_type=f32)
    return jnp.sum(parts[:3], axis=0, keepdims=True)


def over_sources(lines, kernel):
    return lax.dot_general(lines, kernel[...], (((1,), (1,)), ((), ())), preferred_element_type=f32)


def columns(log_total, parts, growth, scores, shift, kernel, left0, right0, asq, bsq, out, sT, left, right):
    sT[...] = jnp.transpose(scores[...])
    potential, weight, top = source_weights(log_total, parts, growth, shift)
    parts3 = over_sources(rows_of(split3(weight), 16), kernel)
    total = jnp.sum(parts3[:3], axis=0, keepdims=True)
    send_copies(out, top + jnp.log2(total))

    @pl.when(jnp.logical_not(in_range(total)))
    def _():
        left[...] = left0[...]
        right[...] = right0[...]
        set_source(left, potential - asq[...])
        peak, exact = log_sum(left, right)
        send_copies(out, peak + jnp.log2(exact))


def rows(log_total, parts, shift, kernel, left0, right0, asq, bsq, out, left, right):
    potential = FACTOR * (-log_total - merged(parts[...]))
    top = jnp.max(potential)
    total = over_targets(jnp.exp2(potential - top), kernel)
    send_copies(out, shift[...] + top + jnp.log2(total))

    @pl.when(jnp.logical_not(in_range(total)))
    def _():
        left[...] = left0[...]
        right[...] = right0[...]
        set_source(left, -asq[...])
        set_target(right, potential - bsq[...])
        peak, exact = log_sum(right, left)
        send_copies(out, peak + jnp.log2(exact))


def put_blocks(out, carried, logs):
    count, lanes = out.shape[0], out.shape[2]
    progs = carried.shape[0]
    lines = jnp.concatenate([logs[:, d * lanes : (d + 1) * lanes] for d in range(count)], axis=0)
    for d in range(count):
        out[d, :progs, :] = carried[:, d * lanes : (d + 1) * lanes]
        out[d, progs:, :] = lines


def carry(log_total, parts, growth, shift, kernel, sT, left0, right0, asq, fout, out, left, right):
    potential, weight, top = source_weights(log_total, parts, growth, shift)
    fout[...] = potential * UNIT
    progs = sT.shape[0]
    scaled = sT[...].astype(f32) * weight
    high = scaled.astype(bf16)
    low = (scaled - high.astype(f32)).astype(bf16)
    sums = over_sources(jnp.concatenate([high, low, rows_of(split3(weight), 16)], axis=0), kernel)
    total = jnp.sum(sums[2 * progs : 2 * progs + 3], axis=0, keepdims=True)
    put_blocks(out, (sums[:progs] + sums[progs : 2 * progs]) / total, top + jnp.log2(total))

    @pl.when(jnp.logical_not(in_range(total)))
    def _():
        left[...] = left0[...]
        right[...] = right0[...]
        set_source(left, potential - asq[...])
        peak, exact = log_sum(left, right)

        def step(k, sums):
            plan = jnp.exp2(logits(tile_of(left, k), right[...]) - peak).astype(bf16)
            return sums + jnp.dot(tile_of(sT, k), plan, preferred_element_type=f32)

        start = jnp.zeros((progs, right.shape[1]), f32)
        sums = lax.fori_loop(0, left.shape[1] // TILE, step, start)
        put_blocks(out, sums / exact, peak + jnp.log2(exact))


def finish(log_total, parts, g, out):
    count, lanes = parts.shape[0], parts.shape[2]
    progs = parts.shape[1] - count
    g[...] = FACTOR * (-log_total - merged(parts[:, progs:, :])) * UNIT
    me = lax.axis_index("src")
    logs = [parts[d, pl.ds(progs + me, 1), :] for d in range(count)]
    peak = functools.reduce(jnp.maximum, logs)
    weights = [jnp.exp2(line - peak) for line in logs]
    total = sum(weights)
    carried = jnp.zeros((progs, lanes), f32)
    for d in range(count):
        carried = carried + (weights[d] / total) * parts[d, :progs, :]
    out[...] = jnp.broadcast_to(jnp.transpose(carried)[None], out.shape)


VMEM = pl.BlockSpec(memory_space=pltpu.VMEM)


def call(kernel, outs, specs, scratch=(), flops=10**7, name=None):
    return pl.pallas_call(
        kernel,
        out_shape=outs,
        in_specs=specs,
        scratch_shapes=list(scratch),
        compiler_params=pltpu.CompilerParams(vmem_limit_bytes=40 << 20),
        cost_estimate=pl.CostEstimate(flops=flops, bytes_accessed=1 << 20, transcendentals=0),
        name=name,
    )


def exchanged(x, axis):
    return lax.all_to_all(x, axis, 0, 0, tiled=True)


def shards(pcs_source, pcs_target, growth, scores):
    count, size = pcs_source.shape
    progs = scores.shape[1]
    sources, targets = lax.axis_size("src"), lax.axis_size("tgt")
    own = size // sources
    log_sources = math.log2(size * sources)
    log_targets = math.log2(pcs_target.shape[1] * targets)
    scale = math.log2(math.e) / (EPSILON * count)
    shape = jax.ShapeDtypeStruct
    line = shape((1, size), f32)
    operand = shape((DEPTH, size), bf16)
    operands = [pltpu.VMEM((DEPTH, size), bf16), pltpu.VMEM((DEPTH, size), bf16)]
    to_targets, to_sources = shape((targets, 1, size), f32), shape((sources, 1, size), f32)

    local, left, right, asq, bsq, shift, kernel = call(
        functools.partial(first_rows, scale),
        (to_targets, operand, operand, line, line, line, shape((size, size), bf16)),
        [VMEM] * 2,
        [pltpu.VMEM((size, DEPTH), bf16)],
        flops=4 * 10**9,
        name="first_rows",
    )(pcs_source, pcs_target)
    growth = growth.reshape(1, size)
    parts = exchanged(local, "tgt")
    for _ in range(ITERS - 1):
        local, sT = call(
            functools.partial(columns, log_sources),
            (to_sources, shape((progs, size), bf16)),
            [VMEM] * 9,
            operands,
            name="columns",
        )(parts, growth, scores, shift, kernel, left, right, asq, bsq)
        parts = exchanged(local, "src")
        local = call(functools.partial(rows, log_targets), to_targets, [VMEM] * 7, operands, name="rows")(
            parts, shift, kernel, left, right, asq, bsq
        )
        parts = exchanged(local, "tgt")
    potential, blocks = call(
        functools.partial(carry, log_sources),
        (line, shape((sources, progs + sources, own), f32)),
        [VMEM] * 8,
        operands,
        name="carry",
    )(parts, growth, shift, kernel, sT, left, right, asq)
    blocks = exchanged(blocks, "src")
    g, result = call(
        functools.partial(finish, log_targets),
        (shape((sources, own), f32), shape((sources, own, progs), f32)),
        [VMEM],
        name="finish",
    )(blocks)
    transported = exchanged(result, "src")
    return potential.reshape(size), g.reshape(size), transported.reshape(size, progs)


def solution(mesh):
    in_specs = (P(None, "src"), P(None, "tgt"), P("src"), P("src", None))
    out_specs = (P("src"), P("tgt"), P("tgt", None))
    return jax.shard_map(shards, mesh=mesh, in_specs=in_specs, out_specs=out_specs, check_vma=False)
```

```python
import functools
import math

import jax
import jax.numpy as jnp
from jax import lax
from jax.experimental import pallas as pl
from jax.experimental.pallas import tpu as pltpu
from jax.sharding import PartitionSpec as P

ITERS = 2
EPSILON = 0.05
MARGIN = 1.0
FACTOR = MARGIN / (MARGIN + EPSILON)

UNIT = EPSILON * math.log(2.0)
LOW, HIGH = 2.0**-90, 2.0**100
STATIC, DEPTH = 96, 112
TILE = 256
f32, bf16 = jnp.float32, jnp.bfloat16


def split3(v):
    high = v.astype(bf16).astype(f32)
    rest = v - high
    mid = rest.astype(bf16).astype(f32)
    return high, mid, (rest - mid).astype(bf16).astype(f32)


def rows_of(values, count):
    row = lax.broadcasted_iota(jnp.int32, (count, values[0].shape[-1]), 0)
    out = jnp.zeros(row.shape, f32)
    for k, v in enumerate(values):
        out = jnp.where(row == k, v, out)
    return out.astype(bf16)


def set_source(left, u):
    one = jnp.ones_like(u)
    left[STATIC:, :] = rows_of([*split3(u), one, one, one], DEPTH - STATIC)


def set_target(right, v):
    one = jnp.ones_like(v)
    right[STATIC:, :] = rows_of([one, one, one, *split3(v)], DEPTH - STATIC)


def tile_of(ref, k):
    return ref[:, pl.ds(pl.multiple_of(k * TILE, TILE), TILE)]


def logits(first, second):
    return lax.dot_general(first, second, (((0,), (0,)), ((), ())), preferred_element_type=f32)


def log_sum(first, second):
    count = first.shape[1] // TILE

    def peaks(k, peak):
        return jnp.maximum(peak, jnp.max(logits(tile_of(first, k), second[...]), axis=0, keepdims=True))

    peak = lax.fori_loop(0, count, peaks, jnp.full((1, second.shape[1]), -jnp.inf, f32))

    def totals(k, total):
        part = jnp.exp2(logits(tile_of(first, k), second[...]) - peak)
        return total + jnp.sum(part, axis=0, keepdims=True)

    total = lax.fori_loop(0, count, totals, jnp.zeros_like(peak))
    return peak, total


def merged(parts):
    peak = jnp.max(parts, axis=0)
    return peak + jnp.log2(jnp.sum(jnp.exp2(parts - peak[None]), axis=0))


def in_range(total):
    return jnp.logical_and(jnp.min(total) >= LOW, jnp.max(total) <= HIGH)


def send_copies(out, value):
    out[...] = jnp.broadcast_to(value[None], out.shape)


def first_rows(
    scale, xy_ref, out, left, right, asq, bsq, shift, kernel, turned
):
    xp = xy_ref[:32, :]
    xw = xp.astype(f32)
    y = xy_ref[32:, :].astype(f32)
    for k, part in enumerate(split3(y * (2.0 * scale))):
        left[32 * k : 32 * k + 32, :] = xp
        right[32 * k : 32 * k + 32, :] = part.astype(bf16)
    asq[...] = jnp.sum(xw * xw, axis=0, keepdims=True) * scale
    bsq[...] = jnp.sum(y * y, axis=0, keepdims=True) * scale
    set_source(left, -asq[...])
    set_target(right, -bsq[...])
    turned[...] = jnp.transpose(right[...])
    size = xp.shape[1]
    chunk = 512
    for n in range(0, size, chunk):
        part = jnp.dot(turned[:TILE, :], left[:, n : n + chunk], preferred_element_type=f32)
        shift[:, n : n + chunk] = jnp.max(part, axis=0, keepdims=True)
    set_source(left, -asq[...] - shift[...])
    sums = []
    for n in range(0, size, chunk):
        total = jnp.zeros((8, chunk), f32)
        for k in range(0, size, TILE):
            part = jnp.dot(turned[k : k + TILE, :], left[:, n : n + chunk], preferred_element_type=f32)
            part = jnp.exp2(part)
            kernel[k : k + TILE, n : n + chunk] = part.astype(bf16)
            total = total + jnp.sum(part.reshape(TILE // 8, 8, chunk), axis=0)
        sums.append(jnp.sum(total, axis=0, keepdims=True))
    total = jnp.concatenate(sums, axis=1)
    out[...] = shift[...] + jnp.log2(total)

    @pl.when(jnp.logical_not(in_range(total)))
    def _():
        set_source(left, -asq[...])
        peak, exact = log_sum(right, left)
        out[...] = peak + jnp.log2(exact)


def source_weights(log_total, parts, growth, shift):
    rows = merged(parts[...])
    potential = FACTOR * (jnp.log2(growth[...]) - log_total - rows)
    log_weight = potential + shift[...]
    top = jnp.max(log_weight)
    return potential, jnp.exp2(log_weight - top), top


def over_targets(weight, kernel):
    parts = jnp.dot(rows_of(split3(weight), 16), kernel[...], preferred_element_type=f32)
    return jnp.sum(parts[:3], axis=0, keepdims=True)


def over_sources(lines, kernel):
    return lax.dot_general(lines, kernel[...], (((1,), (1,)), ((), ())), preferred_element_type=f32)


def columns(log_total, parts, growth, scores, shift, kernel, left0, right0, asq, bsq, out, sT, left, right):
    sT[...] = jnp.transpose(scores[...])
    potential, weight, top = source_weights(log_total, parts, growth, shift)
    parts3 = over_sources(rows_of(split3(weight), 16), kernel)
    total = jnp.sum(parts3[:3], axis=0, keepdims=True)
    send_copies(out, top + jnp.log2(total))

    @pl.when(jnp.logical_not(in_range(total)))
    def _():
        left[...] = left0[...]
        right[...] = right0[...]
        set_source(left, potential - asq[...])
        peak, exact = log_sum(left, right)
        send_copies(out, peak + jnp.log2(exact))


def rows(log_total, parts, shift, kernel, left0, right0, asq, bsq, out, left, right):
    potential = FACTOR * (-log_total - merged(parts[...]))
    top = jnp.max(potential)
    total = over_targets(jnp.exp2(potential - top), kernel)
    out[...] = shift[...] + top + jnp.log2(total)

    @pl.when(jnp.logical_not(in_range(total)))
    def _():
        left[...] = left0[...]
        right[...] = right0[...]
        set_source(left, -asq[...])
        set_target(right, potential - bsq[...])
        peak, exact = log_sum(right, left)
        out[...] = peak + jnp.log2(exact)


def pair(own, other, out):
    peak = jnp.maximum(own[...], other[...])
    total = jnp.exp2(own[...] - peak) + jnp.exp2(other[...] - peak)
    send_copies(out, peak + jnp.log2(total))


def put_blocks(out, carried, logs):
    count, lanes = out.shape[0], out.shape[2]
    progs = carried.shape[0]
    lines = jnp.concatenate([logs[:, d * lanes : (d + 1) * lanes] for d in range(count)], axis=0)
    for d in range(count):
        out[d, :progs, :] = carried[:, d * lanes : (d + 1) * lanes]
        out[d, progs:, :] = lines


def carry(log_total, parts, growth, shift, kernel, sT, left0, right0, asq, fout, out, left, right):
    potential, weight, top = source_weights(log_total, parts, growth, shift)
    fout[...] = potential * UNIT
    progs = sT.shape[0]
    scaled = sT[...].astype(f32) * weight
    high = scaled.astype(bf16)
    low = (scaled - high.astype(f32)).astype(bf16)
    sums = over_sources(jnp.concatenate([high, low, rows_of(split3(weight), 16)], axis=0), kernel)
    total = jnp.sum(sums[2 * progs : 2 * progs + 3], axis=0, keepdims=True)
    put_blocks(out, (sums[:progs] + sums[progs : 2 * progs]) / total, top + jnp.log2(total))

    @pl.when(jnp.logical_not(in_range(total)))
    def _():
        left[...] = left0[...]
        right[...] = right0[...]
        set_source(left, potential - asq[...])
        peak, exact = log_sum(left, right)

        def step(k, sums):
            plan = jnp.exp2(logits(tile_of(left, k), right[...]) - peak).astype(bf16)
            return sums + jnp.dot(tile_of(sT, k), plan, preferred_element_type=f32)

        start = jnp.zeros((progs, right.shape[1]), f32)
        sums = lax.fori_loop(0, left.shape[1] // TILE, step, start)
        put_blocks(out, sums / exact, peak + jnp.log2(exact))


def finish(log_total, parts, g, out):
    count, lanes = parts.shape[0], parts.shape[2]
    progs = parts.shape[1] - count
    g[...] = FACTOR * (-log_total - merged(parts[:, progs:, :])) * UNIT
    me = lax.axis_index("src")
    logs = [parts[d, pl.ds(progs + me, 1), :] for d in range(count)]
    peak = functools.reduce(jnp.maximum, logs)
    weights = [jnp.exp2(line - peak) for line in logs]
    total = sum(weights)
    carried = jnp.zeros((progs, lanes), f32)
    for d in range(count):
        carried = carried + (weights[d] / total) * parts[d, :progs, :]
    out[...] = jnp.broadcast_to(jnp.transpose(carried)[None], out.shape)


VMEM = pl.BlockSpec(memory_space=pltpu.VMEM)


def call(kernel, outs, specs, scratch=(), flops=10**7, name=None):
    return pl.pallas_call(
        kernel,
        out_shape=outs,
        in_specs=specs,
        scratch_shapes=list(scratch),
        compiler_params=pltpu.CompilerParams(vmem_limit_bytes=40 << 20),
        cost_estimate=pl.CostEstimate(flops=flops, bytes_accessed=1 << 20, transcendentals=0),
        name=name,
    )


def exchanged(x, axis, groups=None):
    return lax.all_to_all(x, axis, 0, 0, tiled=True, axis_index_groups=groups)


def rows_exchanged(line, targets):
    other = lax.ppermute(line, "tgt", [(k, k ^ 1) for k in range(targets)])
    copies = jax.ShapeDtypeStruct((targets // 2, *line.shape), f32)
    merged_line = call(pair, copies, [VMEM] * 2, name="pair")(line, other)
    chips = [[2 * z + core for z in range(targets // 2)] for core in range(2)]
    return exchanged(merged_line, "tgt", chips)


def shards(pcs_source, pcs_target, growth, scores):
    count, size = pcs_source.shape
    progs = scores.shape[1]
    sources, targets = lax.axis_size("src"), lax.axis_size("tgt")
    own = size // sources
    log_sources = math.log2(size * sources)
    log_targets = math.log2(pcs_target.shape[1] * targets)
    scale = math.log2(math.e) / (EPSILON * count)
    shape = jax.ShapeDtypeStruct
    line = shape((1, size), f32)
    operand = shape((DEPTH, size), bf16)
    operands = [pltpu.VMEM((DEPTH, size), bf16), pltpu.VMEM((DEPTH, size), bf16)]
    to_sources = shape((sources, 1, size), f32)

    pad = jnp.zeros((32 - count, size), bf16)
    local, left, right, asq, bsq, shift, kernel = call(
        functools.partial(first_rows, scale),
        (line, operand, operand, line, line, line, shape((size, size), bf16)),
        [VMEM],
        [pltpu.VMEM((size, DEPTH), bf16)],
        flops=4 * 10**9,
        name="first_rows",
    )(jnp.concatenate([pcs_source, pad, pcs_target, pad]))
    growth = growth.reshape(1, size)
    parts = rows_exchanged(local, targets)
    for _ in range(ITERS - 1):
        local, sT = call(
            functools.partial(columns, log_sources),
            (to_sources, shape((progs, size), bf16)),
            [VMEM] * 9,
            operands,
            name="columns",
        )(parts, growth, scores, shift, kernel, left, right, asq, bsq)
        parts = exchanged(local, "src")
        local = call(functools.partial(rows, log_targets), line, [VMEM] * 7, operands, name="rows")(
            parts, shift, kernel, left, right, asq, bsq
        )
        parts = rows_exchanged(local, targets)
    potential, blocks = call(
        functools.partial(carry, log_sources),
        (line, shape((sources, progs + sources, own), f32)),
        [VMEM] * 8,
        operands,
        name="carry",
    )(parts, growth, shift, kernel, sT, left, right, asq)
    blocks = exchanged(blocks, "src")
    g, result = call(
        functools.partial(finish, log_targets),
        (shape((sources, own), f32), shape((sources, own, progs), f32)),
        [VMEM],
        name="finish",
    )(blocks)
    transported = exchanged(result, "src")
    return potential.reshape(size), g.reshape(size), transported.reshape(size, progs)


def solution(mesh):
    in_specs = (P(None, "src"), P(None, "tgt"), P("src"), P("src", None))
    out_specs = (P("src"), P("tgt"), P("tgt", None))
    return jax.shard_map(shards, mesh=mesh, in_specs=in_specs, out_specs=out_specs, check_vma=False)
```

```python
import functools
import math

import jax
import jax.numpy as jnp
from jax import lax
from jax.experimental import pallas as pl
from jax.experimental.pallas import tpu as pltpu
from jax.sharding import PartitionSpec as P

ITERS = 2
EPSILON = 0.05
MARGIN = 1.0
FACTOR = MARGIN / (MARGIN + EPSILON)

UNIT = EPSILON * math.log(2.0)
LOW, HIGH, LEAST = 2.0**-90, 2.0**100, 2.0**-100
STATIC, DEPTH = 96, 112
TILE = 256
f32, bf16 = jnp.float32, jnp.bfloat16


def split3(v):
    high = v.astype(bf16).astype(f32)
    rest = v - high
    mid = rest.astype(bf16).astype(f32)
    return high, mid, (rest - mid).astype(bf16).astype(f32)


def rows_of(values, count):
    row = lax.broadcasted_iota(jnp.int32, (count, values[0].shape[-1]), 0)
    out = jnp.zeros(row.shape, f32)
    for k, v in enumerate(values):
        out = jnp.where(row == k, v, out)
    return out.astype(bf16)


def set_source(left, u):
    one = jnp.ones_like(u)
    left[STATIC:, :] = rows_of([*split3(u), one, one, one], DEPTH - STATIC)


def set_target(right, v):
    one = jnp.ones_like(v)
    right[STATIC:, :] = rows_of([one, one, one, *split3(v)], DEPTH - STATIC)


def tile_of(ref, k):
    return ref[:, pl.ds(pl.multiple_of(k * TILE, TILE), TILE)]


def logits(first, second):
    return lax.dot_general(first, second, (((0,), (0,)), ((), ())), preferred_element_type=f32)


def log_sum(first, second):
    count = first.shape[1] // TILE

    def peaks(k, peak):
        return jnp.maximum(peak, jnp.max(logits(tile_of(first, k), second[...]), axis=0, keepdims=True))

    peak = lax.fori_loop(0, count, peaks, jnp.full((1, second.shape[1]), -jnp.inf, f32))

    def totals(k, total):
        part = jnp.exp2(logits(tile_of(first, k), second[...]) - peak)
        return total + jnp.sum(part, axis=0, keepdims=True)

    total = lax.fori_loop(0, count, totals, jnp.zeros_like(peak))
    return peak, total


def merged(parts):
    peak = jnp.max(parts, axis=0)
    return peak + jnp.log2(jnp.sum(jnp.exp2(parts - peak[None]), axis=0))


def in_range(total, weight=None):
    fine = jnp.logical_and(jnp.min(total) >= LOW, jnp.max(total) <= HIGH)
    return fine if weight is None else jnp.logical_and(fine, jnp.min(weight) >= LEAST)


def send_copies(out, value):
    out[...] = jnp.broadcast_to(value[None], out.shape)


def first_rows(
    scale, xy_ref, out, left, right, asq, bsq, shift, kernel, across, turned
):
    xp = xy_ref[:32, :]
    xw = xp.astype(f32)
    y = xy_ref[32:, :].astype(f32)
    for k, part in enumerate(split3(y * (2.0 * scale))):
        left[32 * k : 32 * k + 32, :] = xp
        right[32 * k : 32 * k + 32, :] = part.astype(bf16)
    asq[...] = jnp.sum(xw * xw, axis=0, keepdims=True) * scale
    bsq[...] = jnp.sum(y * y, axis=0, keepdims=True) * scale
    set_source(left, -asq[...])
    set_target(right, -bsq[...])
    turned[...] = jnp.transpose(right[...])
    size = xp.shape[1]
    chunk = 512
    for n in range(0, size, chunk):
        part = jnp.dot(turned[:TILE, :], left[:, n : n + chunk], preferred_element_type=f32)
        shift[:, n : n + chunk] = jnp.max(part, axis=0, keepdims=True)
    set_source(left, -asq[...] - shift[...])
    sums = []
    for n in range(0, size, chunk):
        total = jnp.zeros((8, chunk), f32)
        for k in range(0, size, TILE):
            part = jnp.dot(turned[k : k + TILE, :], left[:, n : n + chunk], preferred_element_type=f32)
            part = jnp.exp2(part)
            low = part.astype(bf16)
            across[k : k + TILE, n : n + chunk] = low
            kernel[n : n + chunk, k : k + TILE] = jnp.transpose(low)
            total = total + jnp.sum(part.reshape(TILE // 8, 8, chunk), axis=0)
        sums.append(jnp.sum(total, axis=0, keepdims=True))
    total = jnp.concatenate(sums, axis=1)
    out[...] = shift[...] + jnp.log2(total)

    @pl.when(jnp.logical_not(in_range(total)))
    def _():
        set_source(left, -asq[...])
        peak, exact = log_sum(right, left)
        out[...] = peak + jnp.log2(exact)


def source_weights(log_total, parts, growth, shift):
    rows = merged(parts[...])
    potential = FACTOR * (jnp.log2(growth[...]) - log_total - rows)
    log_weight = potential + shift[...]
    top = jnp.max(log_weight)
    return potential, jnp.exp2(log_weight - top), top


def weighted(lines, kernel):
    return jnp.dot(lines, kernel[...], preferred_element_type=f32)


def over_first(weight, kernel):
    return jnp.sum(weighted(rows_of(split3(weight), 16), kernel)[:3], axis=0, keepdims=True)


def columns(log_total, parts, growth, scores, shift, kernel, left0, right0, asq, bsq, out, sT, left, right):
    sT[...] = jnp.transpose(scores[...])
    potential, weight, top = source_weights(log_total, parts, growth, shift)
    total = over_first(weight, kernel)
    send_copies(out, top + jnp.log2(total))

    @pl.when(jnp.logical_not(in_range(total, weight)))
    def _():
        left[...] = left0[...]
        right[...] = right0[...]
        set_source(left, potential - asq[...])
        peak, exact = log_sum(left, right)
        send_copies(out, peak + jnp.log2(exact))


def rows(log_total, parts, shift, across, left0, right0, asq, bsq, out, left, right):
    potential = FACTOR * (-log_total - merged(parts[...]))
    top = jnp.max(potential)
    weight = jnp.exp2(potential - top)
    total = over_first(weight, across)
    out[...] = shift[...] + top + jnp.log2(total)

    @pl.when(jnp.logical_not(in_range(total, weight)))
    def _():
        left[...] = left0[...]
        right[...] = right0[...]
        set_source(left, -asq[...])
        set_target(right, potential - bsq[...])
        peak, exact = log_sum(right, left)
        out[...] = peak + jnp.log2(exact)


def pair(own, other, out):
    peak = jnp.maximum(own[...], other[...])
    total = jnp.exp2(own[...] - peak) + jnp.exp2(other[...] - peak)
    send_copies(out, peak + jnp.log2(total))


def put_blocks(out, carried, logs):
    count, lanes = out.shape[0], out.shape[2]
    progs = carried.shape[0]
    lines = jnp.concatenate([logs[:, d * lanes : (d + 1) * lanes] for d in range(count)], axis=0)
    for d in range(count):
        out[d, :progs, :] = carried[:, d * lanes : (d + 1) * lanes]
        out[d, progs:, :] = lines


def carry(log_total, parts, growth, shift, kernel, sT, left0, right0, asq, fout, out, left, right):
    potential, weight, top = source_weights(log_total, parts, growth, shift)
    fout[...] = potential * UNIT
    progs = sT.shape[0]
    scaled = sT[...].astype(f32) * weight
    high = scaled.astype(bf16)
    low = (scaled - high.astype(f32)).astype(bf16)
    sums = weighted(jnp.concatenate([high, low, rows_of(split3(weight), 16)], axis=0), kernel)
    total = jnp.sum(sums[2 * progs : 2 * progs + 3], axis=0, keepdims=True)
    put_blocks(out, (sums[:progs] + sums[progs : 2 * progs]) / total, top + jnp.log2(total))

    @pl.when(jnp.logical_not(in_range(total, weight)))
    def _():
        left[...] = left0[...]
        right[...] = right0[...]
        set_source(left, potential - asq[...])
        peak, exact = log_sum(left, right)

        def step(k, sums):
            plan = jnp.exp2(logits(tile_of(left, k), right[...]) - peak).astype(bf16)
            return sums + jnp.dot(tile_of(sT, k), plan, preferred_element_type=f32)

        start = jnp.zeros((progs, right.shape[1]), f32)
        sums = lax.fori_loop(0, left.shape[1] // TILE, step, start)
        put_blocks(out, sums / exact, peak + jnp.log2(exact))


def finish(log_total, parts, g, out):
    count, lanes = parts.shape[0], parts.shape[2]
    progs = parts.shape[1] - count
    g[...] = FACTOR * (-log_total - merged(parts[:, progs:, :])) * UNIT
    me = lax.axis_index("src")
    logs = [parts[d, pl.ds(progs + me, 1), :] for d in range(count)]
    peak = functools.reduce(jnp.maximum, logs)
    weights = [jnp.exp2(line - peak) for line in logs]
    total = sum(weights)
    carried = jnp.zeros((progs, lanes), f32)
    for d in range(count):
        carried = carried + (weights[d] / total) * parts[d, :progs, :]
    out[...] = jnp.broadcast_to(jnp.transpose(carried)[None], out.shape)


VMEM = pl.BlockSpec(memory_space=pltpu.VMEM)


def call(kernel, outs, specs, scratch=(), flops=10**7, name=None):
    return pl.pallas_call(
        kernel,
        out_shape=outs,
        in_specs=specs,
        scratch_shapes=list(scratch),
        compiler_params=pltpu.CompilerParams(vmem_limit_bytes=24 << 20),
        cost_estimate=pl.CostEstimate(flops=flops, bytes_accessed=1 << 20, transcendentals=0),
        name=name,
    )


def exchanged(x, axis, groups=None):
    return lax.all_to_all(x, axis, 0, 0, tiled=True, axis_index_groups=groups)


def rows_exchanged(line, targets):
    other = lax.ppermute(line, "tgt", [(k, k ^ 1) for k in range(targets)])
    copies = jax.ShapeDtypeStruct((targets // 2, *line.shape), f32)
    merged_line = call(pair, copies, [VMEM] * 2, name="pair")(line, other)
    chips = [[2 * z + core for z in range(targets // 2)] for core in range(2)]
    return exchanged(merged_line, "tgt", chips)


def shards(pcs_source, pcs_target, growth, scores):
    count, size = pcs_source.shape
    progs = scores.shape[1]
    sources, targets = lax.axis_size("src"), lax.axis_size("tgt")
    own = size // sources
    log_sources = math.log2(size * sources)
    log_targets = math.log2(pcs_target.shape[1] * targets)
    scale = math.log2(math.e) / (EPSILON * count)
    shape = jax.ShapeDtypeStruct
    line = shape((1, size), f32)
    square = shape((size, size), bf16)
    operand = shape((DEPTH, size), bf16)
    operands = [pltpu.VMEM((DEPTH, size), bf16), pltpu.VMEM((DEPTH, size), bf16)]
    to_sources = shape((sources, 1, size), f32)

    pad = jnp.zeros((32 - count, size), bf16)
    local, left, right, asq, bsq, shift, kernel, across = call(
        functools.partial(first_rows, scale),
        (line, operand, operand, line, line, line, square, square),
        [VMEM],
        [pltpu.VMEM((size, DEPTH), bf16)],
        flops=4 * 10**9,
        name="first_rows",
    )(jnp.concatenate([pcs_source, pad, pcs_target, pad]))
    growth = growth.reshape(1, size)
    parts = rows_exchanged(local, targets)
    for _ in range(ITERS - 1):
        local, sT = call(
            functools.partial(columns, log_sources),
            (to_sources, shape((progs, size), bf16)),
            [VMEM] * 9,
            operands,
            name="columns",
        )(parts, growth, scores, shift, kernel, left, right, asq, bsq)
        parts = exchanged(local, "src")
        local = call(functools.partial(rows, log_targets), line, [VMEM] * 7, operands, name="rows")(
            parts, shift, across, left, right, asq, bsq
        )
        parts = rows_exchanged(local, targets)
    potential, blocks = call(
        functools.partial(carry, log_sources),
        (line, shape((sources, progs + sources, own), f32)),
        [VMEM] * 8,
        operands,
        name="carry",
    )(parts, growth, shift, kernel, sT, left, right, asq)
    blocks = exchanged(blocks, "src")
    g, result = call(
        functools.partial(finish, log_targets),
        (shape((sources, own), f32), shape((sources, own, progs), f32)),
        [VMEM],
        name="finish",
    )(blocks)
    transported = exchanged(result, "src")
    return potential.reshape(size), g.reshape(size), transported.reshape(size, progs)


def solution(mesh):
    in_specs = (P(None, "src"), P(None, "tgt"), P("src"), P("src", None))
    out_specs = (P("src"), P("tgt"), P("tgt", None))
    return jax.shard_map(shards, mesh=mesh, in_specs=in_specs, out_specs=out_specs, check_vma=False)
```

```python
import functools
import math

import jax
import jax.numpy as jnp
from jax import lax
from jax.experimental import pallas as pl
from jax.experimental.pallas import tpu as pltpu
from jax.sharding import PartitionSpec as P

ITERS = 2
EPSILON = 0.05
MARGIN = 1.0
FACTOR = MARGIN / (MARGIN + EPSILON)

UNIT = EPSILON * math.log(2.0)
LOW, HIGH, LEAST = 2.0**-90, 2.0**100, 2.0**-100
STATIC, DEPTH = 96, 112
TILE = 256
f32, bf16 = jnp.float32, jnp.bfloat16


def split3(v):
    high = v.astype(bf16).astype(f32)
    rest = v - high
    mid = rest.astype(bf16).astype(f32)
    return high, mid, (rest - mid).astype(bf16).astype(f32)


def rows_of(values, count):
    row = lax.broadcasted_iota(jnp.int32, (count, values[0].shape[-1]), 0)
    out = jnp.zeros(row.shape, f32)
    for k, v in enumerate(values):
        out = jnp.where(row == k, v, out)
    return out.astype(bf16)


def set_source(left, u):
    one = jnp.ones_like(u)
    left[STATIC:, :] = rows_of([*split3(u), one, one, one], DEPTH - STATIC)


def set_target(right, v):
    one = jnp.ones_like(v)
    right[STATIC:, :] = rows_of([one, one, one, *split3(v)], DEPTH - STATIC)


def tile_of(ref, k):
    return ref[:, pl.ds(pl.multiple_of(k * TILE, TILE), TILE)]


def logits(first, second):
    return lax.dot_general(first, second, (((0,), (0,)), ((), ())), preferred_element_type=f32)


def log_sum(first, second):
    count = first.shape[1] // TILE

    def peaks(k, peak):
        return jnp.maximum(peak, jnp.max(logits(tile_of(first, k), second[...]), axis=0, keepdims=True))

    peak = lax.fori_loop(0, count, peaks, jnp.full((1, second.shape[1]), -jnp.inf, f32))

    def totals(k, total):
        part = jnp.exp2(logits(tile_of(first, k), second[...]) - peak)
        return total + jnp.sum(part, axis=0, keepdims=True)

    total = lax.fori_loop(0, count, totals, jnp.zeros_like(peak))
    return peak, total


def merged(parts):
    peak = jnp.max(parts, axis=0)
    return peak + jnp.log2(jnp.sum(jnp.exp2(parts - peak[None]), axis=0))


def in_range(total, weight=None):
    fine = jnp.logical_and(jnp.min(total) >= LOW, jnp.max(total) <= HIGH)
    return fine if weight is None else jnp.logical_and(fine, jnp.min(weight) >= LEAST)


def send_copies(out, value):
    out[...] = jnp.broadcast_to(value[None], out.shape)


def first_rows(
    scale, xy_ref, out, left, right, asq, bsq, shift, kernel, across, turned
):
    xp = xy_ref[:32, :]
    xw = xp.astype(f32)
    y = xy_ref[32:, :].astype(f32)
    for k, part in enumerate(split3(y * (2.0 * scale))):
        left[32 * k : 32 * k + 32, :] = xp
        right[32 * k : 32 * k + 32, :] = part.astype(bf16)
    asq[...] = jnp.sum(xw * xw, axis=0, keepdims=True) * scale
    bsq[...] = jnp.sum(y * y, axis=0, keepdims=True) * scale
    set_source(left, -asq[...])
    set_target(right, -bsq[...])
    turned[...] = jnp.transpose(right[...])
    size = xp.shape[1]
    chunk = 512
    for n in range(0, size, chunk):
        part = jnp.dot(turned[:TILE, :], left[:, n : n + chunk], preferred_element_type=f32)
        shift[:, n : n + chunk] = jnp.max(part, axis=0, keepdims=True)
    set_source(left, -asq[...] - shift[...])
    sums = []
    for n in range(0, size, chunk):
        total = jnp.zeros((8, chunk), f32)
        for k in range(0, size, TILE):
            part = jnp.dot(turned[k : k + TILE, :], left[:, n : n + chunk], preferred_element_type=f32)
            part = jnp.exp2(part)
            low = part.astype(bf16)
            across[k : k + TILE, n : n + chunk] = low
            kernel[n : n + chunk, k : k + TILE] = jnp.transpose(low)
            total = total + jnp.sum(part.reshape(TILE // 8, 8, chunk), axis=0)
        sums.append(jnp.sum(total, axis=0, keepdims=True))
    total = jnp.concatenate(sums, axis=1)
    out[...] = shift[...] + jnp.log2(total)

    @pl.when(jnp.logical_not(in_range(total)))
    def _():
        set_source(left, -asq[...])
        peak, exact = log_sum(right, left)
        out[...] = peak + jnp.log2(exact)


def source_weights(log_total, parts, growth, shift):
    rows = merged(parts[...])
    potential = FACTOR * (jnp.log2(growth[...]) - log_total - rows)
    log_weight = potential + shift[...]
    top = jnp.max(log_weight)
    return potential, jnp.exp2(log_weight - top), top


def weighted(lines, kernel):
    return jnp.dot(lines, kernel[...], preferred_element_type=f32)


def over_first(weight, kernel):
    return jnp.sum(weighted(rows_of(split3(weight), 16), kernel)[:3], axis=0, keepdims=True)


def columns(log_total, parts, growth, scores, shift, kernel, left0, right0, asq, bsq, out, sT, left, right):
    sT[...] = jnp.transpose(scores[...])
    potential, weight, top = source_weights(log_total, parts, growth, shift)
    total = over_first(weight, kernel)
    send_copies(out, top + jnp.log2(total))

    @pl.when(jnp.logical_not(in_range(total, weight)))
    def _():
        left[...] = left0[...]
        right[...] = right0[...]
        set_source(left, potential - asq[...])
        peak, exact = log_sum(left, right)
        send_copies(out, peak + jnp.log2(exact))


def rows(log_total, parts, shift, across, left0, right0, asq, bsq, out, left, right):
    potential = FACTOR * (-log_total - merged(parts[...]))
    top = jnp.max(potential)
    weight = jnp.exp2(potential - top)
    total = over_first(weight, across)
    out[...] = shift[...] + top + jnp.log2(total)

    @pl.when(jnp.logical_not(in_range(total, weight)))
    def _():
        left[...] = left0[...]
        right[...] = right0[...]
        set_source(left, -asq[...])
        set_target(right, potential - bsq[...])
        peak, exact = log_sum(right, left)
        out[...] = peak + jnp.log2(exact)


def pair(own, other, out):
    peak = jnp.maximum(own[...], other[...])
    total = jnp.exp2(own[...] - peak) + jnp.exp2(other[...] - peak)
    send_copies(out, peak + jnp.log2(total))


def put_blocks(out, carried, logs):
    count, lanes = out.shape[0], out.shape[2]
    progs = carried.shape[0]
    lines = jnp.concatenate([logs[:, d * lanes : (d + 1) * lanes] for d in range(count)], axis=0)
    for d in range(count):
        out[d, :progs, :] = carried[:, d * lanes : (d + 1) * lanes]
        out[d, progs:, :] = lines


def carry(log_total, parts, growth, shift, kernel, sT, left0, right0, asq, fout, out, left, right):
    potential, weight, top = source_weights(log_total, parts, growth, shift)
    fout[...] = potential * UNIT
    progs = sT.shape[0]
    scaled = sT[...].astype(f32) * weight
    high = scaled.astype(bf16)
    low = (scaled - high.astype(f32)).astype(bf16)
    sums = weighted(jnp.concatenate([high, low, rows_of(split3(weight), 16)], axis=0), kernel)
    total = jnp.sum(sums[2 * progs : 2 * progs + 3], axis=0, keepdims=True)
    put_blocks(out, (sums[:progs] + sums[progs : 2 * progs]) / total, top + jnp.log2(total))

    @pl.when(jnp.logical_not(in_range(total, weight)))
    def _():
        left[...] = left0[...]
        right[...] = right0[...]
        set_source(left, potential - asq[...])
        peak, exact = log_sum(left, right)

        def step(k, sums):
            plan = jnp.exp2(logits(tile_of(left, k), right[...]) - peak).astype(bf16)
            return sums + jnp.dot(tile_of(sT, k), plan, preferred_element_type=f32)

        start = jnp.zeros((progs, right.shape[1]), f32)
        sums = lax.fori_loop(0, left.shape[1] // TILE, step, start)
        put_blocks(out, sums / exact, peak + jnp.log2(exact))


def finish(log_total, parts, g, out):
    count, lanes = parts.shape[0], parts.shape[2]
    progs = parts.shape[1] - count
    g[...] = FACTOR * (-log_total - merged(parts[:, progs:, :])) * UNIT
    me = place_in_skewed(count)
    logs = [parts[d, pl.ds(progs + me, 1), :] for d in range(count)]
    peak = functools.reduce(jnp.maximum, logs)
    weights = [jnp.exp2(line - peak) for line in logs]
    total = sum(weights)
    carried = jnp.zeros((progs, lanes), f32)
    for d in range(count):
        carried = carried + (weights[d] / total) * parts[d, :progs, :]
    out[...] = jnp.broadcast_to(jnp.transpose(carried)[None], out.shape)


VMEM = pl.BlockSpec(memory_space=pltpu.VMEM)


def call(kernel, outs, specs, scratch=(), flops=10**7, name=None):
    return pl.pallas_call(
        kernel,
        out_shape=outs,
        in_specs=specs,
        scratch_shapes=list(scratch),
        compiler_params=pltpu.CompilerParams(vmem_limit_bytes=24 << 20),
        cost_estimate=pl.CostEstimate(flops=flops, bytes_accessed=1 << 20, transcendentals=0),
        name=name,
    )


def exchanged(x, axis, groups=None):
    return lax.all_to_all(x, axis, 0, 0, tiled=True, axis_index_groups=groups)


def rows_exchanged(line, targets):
    other = lax.ppermute(line, "tgt", [(k, k ^ 1) for k in range(targets)])
    copies = jax.ShapeDtypeStruct((targets // 2, *line.shape), f32)
    merged_line = call(pair, copies, [VMEM] * 2, name="pair")(line, other)
    chips = [[2 * z + core for z in range(targets // 2)] for core in range(2)]
    return exchanged(merged_line, "tgt", chips)


def skewed(sources):
    side = math.isqrt(sources)
    return [[(p // side) * side + (p + p // side) % side for p in range(sources)]]


def place_in_skewed(sources):
    side = math.isqrt(sources)
    me = lax.axis_index("src")
    y, x = me // side, me % side
    return y * side + (x - y + side) % side


def shards(pcs_source, pcs_target, growth, scores):
    count, size = pcs_source.shape
    progs = scores.shape[1]
    sources, targets = lax.axis_size("src"), lax.axis_size("tgt")
    own = size // sources
    log_sources = math.log2(size * sources)
    log_targets = math.log2(pcs_target.shape[1] * targets)
    scale = math.log2(math.e) / (EPSILON * count)
    shape = jax.ShapeDtypeStruct
    line = shape((1, size), f32)
    square = shape((size, size), bf16)
    operand = shape((DEPTH, size), bf16)
    operands = [pltpu.VMEM((DEPTH, size), bf16), pltpu.VMEM((DEPTH, size), bf16)]
    to_sources = shape((sources, 1, size), f32)

    pad = jnp.zeros((32 - count, size), bf16)
    local, left, right, asq, bsq, shift, kernel, across = call(
        functools.partial(first_rows, scale),
        (line, operand, operand, line, line, line, square, square),
        [VMEM],
        [pltpu.VMEM((size, DEPTH), bf16)],
        flops=4 * 10**9,
        name="first_rows",
    )(jnp.concatenate([pcs_source, pad, pcs_target, pad]))
    growth = growth.reshape(1, size)
    parts = rows_exchanged(local, targets)
    for _ in range(ITERS - 1):
        local, sT = call(
            functools.partial(columns, log_sources),
            (to_sources, shape((progs, size), bf16)),
            [VMEM] * 9,
            operands,
            name="columns",
        )(parts, growth, scores, shift, kernel, left, right, asq, bsq)
        parts = exchanged(local, "src", skewed(sources))
        local = call(functools.partial(rows, log_targets), line, [VMEM] * 7, operands, name="rows")(
            parts, shift, across, left, right, asq, bsq
        )
        parts = rows_exchanged(local, targets)
    potential, blocks = call(
        functools.partial(carry, log_sources),
        (line, shape((sources, progs + sources, own), f32)),
        [VMEM] * 8,
        operands,
        name="carry",
    )(parts, growth, shift, kernel, sT, left, right, asq)
    blocks = exchanged(blocks, "src", skewed(sources))
    g, result = call(
        functools.partial(finish, log_targets),
        (shape((sources, own), f32), shape((sources, own, progs), f32)),
        [VMEM],
        name="finish",
    )(blocks)
    transported = exchanged(result, "src", skewed(sources))
    return potential.reshape(size), g.reshape(size), transported.reshape(size, progs)


def solution(mesh):
    in_specs = (P(None, "src"), P(None, "tgt"), P("src"), P("src", None))
    out_specs = (P("src"), P("tgt"), P("tgt", None))
    return jax.shard_map(shards, mesh=mesh, in_specs=in_specs, out_specs=out_specs, check_vma=False)
```

```python
import functools
import math

import jax
import jax.numpy as jnp
from jax import lax
from jax.experimental import pallas as pl
from jax.experimental.pallas import tpu as pltpu
from jax.sharding import PartitionSpec as P

ITERS = 2
EPSILON = 0.05
MARGIN = 1.0
FACTOR = MARGIN / (MARGIN + EPSILON)

UNIT = EPSILON * math.log(2.0)
LOW, HIGH, LEAST = 2.0**-90, 2.0**100, 2.0**-100
STATIC, DEPTH = 96, 112
TILE, SAMPLE = 256, 64
f32, bf16 = jnp.float32, jnp.bfloat16


def split3(v):
    high = v.astype(bf16).astype(f32)
    rest = v - high
    mid = rest.astype(bf16).astype(f32)
    return high, mid, (rest - mid).astype(bf16).astype(f32)


def rows_of(values, count):
    row = lax.broadcasted_iota(jnp.int32, (count, values[0].shape[-1]), 0)
    out = jnp.zeros(row.shape, f32)
    for k, v in enumerate(values):
        out = jnp.where(row == k, v, out)
    return out.astype(bf16)


def set_source(left, u):
    one = jnp.ones_like(u)
    left[STATIC:, :] = rows_of([*split3(u), one, one, one], DEPTH - STATIC)


def set_target(right, v):
    one = jnp.ones_like(v)
    right[STATIC:, :] = rows_of([one, one, one, *split3(v)], DEPTH - STATIC)


def tile_of(ref, k):
    return ref[:, pl.ds(pl.multiple_of(k * TILE, TILE), TILE)]


def logits(first, second):
    return lax.dot_general(first, second, (((0,), (0,)), ((), ())), preferred_element_type=f32)


def log_sum(first, second):
    count = first.shape[1] // TILE

    def peaks(k, peak):
        return jnp.maximum(peak, jnp.max(logits(tile_of(first, k), second[...]), axis=0, keepdims=True))

    peak = lax.fori_loop(0, count, peaks, jnp.full((1, second.shape[1]), -jnp.inf, f32))

    def totals(k, total):
        part = jnp.exp2(logits(tile_of(first, k), second[...]) - peak)
        return total + jnp.sum(part, axis=0, keepdims=True)

    total = lax.fori_loop(0, count, totals, jnp.zeros_like(peak))
    return peak, total


def merged(parts):
    peak = jnp.max(parts, axis=0)
    return peak + jnp.log2(jnp.sum(jnp.exp2(parts - peak[None]), axis=0))


def in_range(total, weight=None):
    fine = jnp.logical_and(jnp.min(total) >= LOW, jnp.max(total) <= HIGH)
    return fine if weight is None else jnp.logical_and(fine, jnp.min(weight) >= LEAST)


def send_copies(out, value):
    out[...] = jnp.broadcast_to(value[None], out.shape)


def first_rows(
    scale, xy_ref, out, left, right, asq, bsq, shift, kernel, across, turned
):
    xp = xy_ref[:32, :]
    xw = xp.astype(f32)
    y = xy_ref[32:, :].astype(f32)
    for k, part in enumerate(split3(y * (2.0 * scale))):
        left[32 * k : 32 * k + 32, :] = xp
        right[32 * k : 32 * k + 32, :] = part.astype(bf16)
    asq[...] = jnp.sum(xw * xw, axis=0, keepdims=True) * scale
    bsq[...] = jnp.sum(y * y, axis=0, keepdims=True) * scale
    set_source(left, -asq[...])
    set_target(right, -bsq[...])
    turned[...] = jnp.transpose(right[...])
    size = xp.shape[1]
    chunk = 512
    for n in range(0, size, chunk):
        part = jnp.dot(turned[:SAMPLE, :], left[:, n : n + chunk], preferred_element_type=f32)
        shift[:, n : n + chunk] = jnp.max(part, axis=0, keepdims=True)
    set_source(left, -asq[...] - shift[...])
    sums = []
    for n in range(0, size, chunk):
        total = jnp.zeros((8, chunk), f32)
        for k in range(0, size, TILE):
            part = jnp.dot(turned[k : k + TILE, :], left[:, n : n + chunk], preferred_element_type=f32)
            part = jnp.exp2(part)
            low = part.astype(bf16)
            across[k : k + TILE, n : n + chunk] = low
            kernel[n : n + chunk, k : k + TILE] = jnp.transpose(low)
            total = total + jnp.sum(part.reshape(TILE // 8, 8, chunk), axis=0)
        sums.append(jnp.sum(total, axis=0, keepdims=True))
    total = jnp.concatenate(sums, axis=1)
    out[...] = shift[...] + jnp.log2(total)

    @pl.when(jnp.logical_not(in_range(total)))
    def _():
        set_source(left, -asq[...])
        peak, exact = log_sum(right, left)
        out[...] = peak + jnp.log2(exact)


def source_weights(log_total, parts, growth, shift):
    rows = merged(parts[...])
    potential = FACTOR * (jnp.log2(growth[...]) - log_total - rows)
    log_weight = potential + shift[...]
    top = jnp.max(log_weight)
    return potential, jnp.exp2(log_weight - top), top


def weighted(lines, kernel):
    return jnp.dot(lines, kernel[...], preferred_element_type=f32)


def over_first(weight, kernel):
    return jnp.sum(weighted(rows_of(split3(weight), 16), kernel)[:3], axis=0, keepdims=True)


def columns(log_total, parts, growth, scores, shift, kernel, left0, right0, asq, bsq, out, sT, left, right):
    sT[...] = jnp.transpose(scores[...])
    potential, weight, top = source_weights(log_total, parts, growth, shift)
    total = over_first(weight, kernel)
    send_copies(out, top + jnp.log2(total))

    @pl.when(jnp.logical_not(in_range(total, weight)))
    def _():
        left[...] = left0[...]
        right[...] = right0[...]
        set_source(left, potential - asq[...])
        peak, exact = log_sum(left, right)
        send_copies(out, peak + jnp.log2(exact))


def rows(log_total, parts, shift, across, left0, right0, asq, bsq, out, left, right):
    potential = FACTOR * (-log_total - merged(parts[...]))
    top = jnp.max(potential)
    weight = jnp.exp2(potential - top)
    total = over_first(weight, across)
    out[...] = shift[...] + top + jnp.log2(total)

    @pl.when(jnp.logical_not(in_range(total, weight)))
    def _():
        left[...] = left0[...]
        right[...] = right0[...]
        set_source(left, -asq[...])
        set_target(right, potential - bsq[...])
        peak, exact = log_sum(right, left)
        out[...] = peak + jnp.log2(exact)


def pair(own, other, out):
    peak = jnp.maximum(own[...], other[...])
    total = jnp.exp2(own[...] - peak) + jnp.exp2(other[...] - peak)
    send_copies(out, peak + jnp.log2(total))


def put_blocks(out, carried, logs):
    count, lanes = out.shape[0], out.shape[2]
    progs = carried.shape[0]
    lines = jnp.concatenate([logs[:, d * lanes : (d + 1) * lanes] for d in range(count)], axis=0)
    for d in range(count):
        out[d, :progs, :] = carried[:, d * lanes : (d + 1) * lanes]
        out[d, progs:, :] = lines


def carry(log_total, parts, growth, shift, kernel, sT, left0, right0, asq, fout, out, left, right):
    potential, weight, top = source_weights(log_total, parts, growth, shift)
    fout[...] = potential * UNIT
    progs = sT.shape[0]
    scaled = sT[...].astype(f32) * weight
    high = scaled.astype(bf16)
    low = (scaled - high.astype(f32)).astype(bf16)
    sums = weighted(jnp.concatenate([high, low, rows_of(split3(weight), 16)], axis=0), kernel)
    total = jnp.sum(sums[2 * progs : 2 * progs + 3], axis=0, keepdims=True)
    put_blocks(out, (sums[:progs] + sums[progs : 2 * progs]) * (1.0 / total), top + jnp.log2(total))

    @pl.when(jnp.logical_not(in_range(total, weight)))
    def _():
        left[...] = left0[...]
        right[...] = right0[...]
        set_source(left, potential - asq[...])
        peak, exact = log_sum(left, right)

        def step(k, sums):
            plan = jnp.exp2(logits(tile_of(left, k), right[...]) - peak).astype(bf16)
            return sums + jnp.dot(tile_of(sT, k), plan, preferred_element_type=f32)

        start = jnp.zeros((progs, right.shape[1]), f32)
        sums = lax.fori_loop(0, left.shape[1] // TILE, step, start)
        put_blocks(out, sums / exact, peak + jnp.log2(exact))


def finish(log_total, parts, g, out):
    count, lanes = parts.shape[0], parts.shape[2]
    progs = parts.shape[1] - count
    g[...] = FACTOR * (-log_total - merged(parts[:, progs:, :])) * UNIT
    me = place_in_skewed(count)
    logs = [parts[d, pl.ds(progs + me, 1), :] for d in range(count)]
    peak = functools.reduce(jnp.maximum, logs)
    weights = [jnp.exp2(line - peak) for line in logs]
    total = sum(weights)
    carried = jnp.zeros((progs, lanes), f32)
    for d in range(count):
        carried = carried + (weights[d] / total) * parts[d, :progs, :]
    out[...] = jnp.broadcast_to(jnp.transpose(carried)[None], out.shape)


VMEM = pl.BlockSpec(memory_space=pltpu.VMEM)


def call(kernel, outs, specs, scratch=(), flops=10**7, name=None):
    return pl.pallas_call(
        kernel,
        out_shape=outs,
        in_specs=specs,
        scratch_shapes=list(scratch),
        compiler_params=pltpu.CompilerParams(vmem_limit_bytes=24 << 20),
        cost_estimate=pl.CostEstimate(flops=flops, bytes_accessed=1 << 20, transcendentals=0),
        name=name,
    )


def exchanged(x, axis, groups=None):
    return lax.all_to_all(x, axis, 0, 0, tiled=True, axis_index_groups=groups)


def rows_exchanged(line, targets):
    other = lax.ppermute(line, "tgt", [(k, k ^ 1) for k in range(targets)])
    copies = jax.ShapeDtypeStruct((targets // 2, *line.shape), f32)
    merged_line = call(pair, copies, [VMEM] * 2, name="pair")(line, other)
    chips = [[2 * ((z // 2 if z % 2 == 0 else targets // 2 - 1 - z // 2)) + core for z in range(targets // 2)] for core in range(2)]
    return exchanged(merged_line, "tgt", chips)


def skewed(sources):
    side = math.isqrt(sources)
    return [[(p // side) * side + (p + p // side) % side for p in range(sources)]]


def place_in_skewed(sources):
    side = math.isqrt(sources)
    me = lax.axis_index("src")
    y, x = me // side, me % side
    return y * side + (x - y + side) % side


def shards(pcs_source, pcs_target, growth, scores):
    count, size = pcs_source.shape
    progs = scores.shape[1]
    sources, targets = lax.axis_size("src"), lax.axis_size("tgt")
    own = size // sources
    log_sources = math.log2(size * sources)
    log_targets = math.log2(pcs_target.shape[1] * targets)
    scale = math.log2(math.e) / (EPSILON * count)
    shape = jax.ShapeDtypeStruct
    line = shape((1, size), f32)
    square = shape((size, size), bf16)
    operand = shape((DEPTH, size), bf16)
    operands = [pltpu.VMEM((DEPTH, size), bf16), pltpu.VMEM((DEPTH, size), bf16)]
    to_sources = shape((sources, 1, size), f32)

    pad = jnp.zeros((32 - count, size), bf16)
    local, left, right, asq, bsq, shift, kernel, across = call(
        functools.partial(first_rows, scale),
        (line, operand, operand, line, line, line, square, square),
        [VMEM],
        [pltpu.VMEM((size, DEPTH), bf16)],
        flops=4 * 10**9,
        name="first_rows",
    )(jnp.concatenate([pcs_source, pad, pcs_target, pad]))
    growth = growth.reshape(1, size)
    parts = rows_exchanged(local, targets)
    for _ in range(ITERS - 1):
        local, sT = call(
            functools.partial(columns, log_sources),
            (to_sources, shape((progs, size), bf16)),
            [VMEM] * 9,
            operands,
            name="columns",
        )(parts, growth, scores, shift, kernel, left, right, asq, bsq)
        parts = exchanged(local, "src", skewed(sources))
        local = call(functools.partial(rows, log_targets), line, [VMEM] * 7, operands, name="rows")(
            parts, shift, across, left, right, asq, bsq
        )
        parts = rows_exchanged(local, targets)
    potential, blocks = call(
        functools.partial(carry, log_sources),
        (line, shape((sources, progs + sources, own), f32)),
        [VMEM] * 8,
        operands,
        name="carry",
    )(parts, growth, shift, kernel, sT, left, right, asq)
    blocks = exchanged(blocks, "src", skewed(sources))
    g, result = call(
        functools.partial(finish, log_targets),
        (shape((sources, own), f32), shape((sources, own, progs), f32)),
        [VMEM],
        name="finish",
    )(blocks)
    transported = exchanged(result, "src", skewed(sources))
    return potential.reshape(size), g.reshape(size), transported.reshape(size, progs)


def solution(mesh):
    in_specs = (P(None, "src"), P(None, "tgt"), P("src"), P("src", None))
    out_specs = (P("src"), P("tgt"), P("tgt", None))
    return jax.shard_map(shards, mesh=mesh, in_specs=in_specs, out_specs=out_specs, check_vma=False)
```

```python
import functools
import math

import jax
import jax.numpy as jnp
from jax import lax
from jax.experimental import pallas as pl
from jax.experimental.pallas import tpu as pltpu
from jax.sharding import PartitionSpec as P

ITERS = 2
EPSILON = 0.05
MARGIN = 1.0
FACTOR = MARGIN / (MARGIN + EPSILON)

UNIT = EPSILON * math.log(2.0)
LOW, HIGH, LEAST = 2.0**-90, 2.0**100, 2.0**-100
STATIC, DEPTH = 96, 112
TILE, SAMPLE = 256, 64
f32, bf16 = jnp.float32, jnp.bfloat16


def split3(v):
    high = v.astype(bf16).astype(f32)
    rest = v - high
    mid = rest.astype(bf16).astype(f32)
    return high, mid, (rest - mid).astype(bf16).astype(f32)


def rows_of(values, count):
    row = lax.broadcasted_iota(jnp.int32, (count, values[0].shape[-1]), 0)
    out = jnp.zeros(row.shape, f32)
    for k, v in enumerate(values):
        out = jnp.where(row == k, v, out)
    return out.astype(bf16)


def set_source(left, u):
    one = jnp.ones_like(u)
    left[STATIC:, :] = rows_of([*split3(u), one, one, one], DEPTH - STATIC)


def set_target(right, v):
    one = jnp.ones_like(v)
    right[STATIC:, :] = rows_of([one, one, one, *split3(v)], DEPTH - STATIC)


def tile_of(ref, k):
    return ref[:, pl.ds(pl.multiple_of(k * TILE, TILE), TILE)]


def logits(first, second):
    return lax.dot_general(first, second, (((0,), (0,)), ((), ())), preferred_element_type=f32)


def log_sum(first, second):
    count = first.shape[1] // TILE

    def peaks(k, peak):
        return jnp.maximum(peak, jnp.max(logits(tile_of(first, k), second[...]), axis=0, keepdims=True))

    peak = lax.fori_loop(0, count, peaks, jnp.full((1, second.shape[1]), -jnp.inf, f32))

    def totals(k, total):
        part = jnp.exp2(logits(tile_of(first, k), second[...]) - peak)
        return total + jnp.sum(part, axis=0, keepdims=True)

    total = lax.fori_loop(0, count, totals, jnp.zeros_like(peak))
    return peak, total


def merged(parts):
    peak = jnp.max(parts, axis=0)
    return peak + jnp.log2(jnp.sum(jnp.exp2(parts - peak[None]), axis=0))


def in_range(total, weight=None):
    fine = jnp.logical_and(jnp.min(total) >= LOW, jnp.max(total) <= HIGH)
    return fine if weight is None else jnp.logical_and(fine, jnp.min(weight) >= LEAST)


def send_copies(out, value):
    out[...] = jnp.broadcast_to(value[None], out.shape)


def first_rows(
    scale, xy_ref, out, left, right, asq, bsq, shift, kernel, across, turned
):
    xp = xy_ref[:32, :]
    xw = xp.astype(f32)
    y = xy_ref[32:, :].astype(f32)
    for k, part in enumerate(split3(y * (2.0 * scale))):
        left[32 * k : 32 * k + 32, :] = xp
        right[32 * k : 32 * k + 32, :] = part.astype(bf16)
    asq[...] = jnp.sum(xw * xw, axis=0, keepdims=True) * scale
    bsq[...] = jnp.sum(y * y, axis=0, keepdims=True) * scale
    set_source(left, -asq[...])
    set_target(right, -bsq[...])
    turned[...] = jnp.transpose(right[...])
    size = xp.shape[1]
    chunk = 512
    for n in range(0, size, chunk):
        part = jnp.dot(turned[:SAMPLE, :], left[:, n : n + chunk], preferred_element_type=f32)
        shift[:, n : n + chunk] = jnp.max(part, axis=0, keepdims=True)
    set_source(left, -asq[...] - shift[...])
    sums = []
    chunk, tile = 256, 512
    for n in range(0, size, chunk):
        total = jnp.zeros((8, chunk), f32)
        for k in range(0, size, tile):
            part = jnp.dot(turned[k : k + tile, :], left[:, n : n + chunk], preferred_element_type=f32)
            part = jnp.exp2(part)
            low = part.astype(bf16)
            across[k : k + tile, n : n + chunk] = low
            kernel[n : n + chunk, k : k + tile] = jnp.transpose(low)
            total = total + jnp.sum(part.reshape(tile // 8, 8, chunk), axis=0)
        sums.append(jnp.sum(total, axis=0, keepdims=True))
    total = jnp.concatenate(sums, axis=1)
    out[...] = shift[...] + jnp.log2(total)

    @pl.when(jnp.logical_not(in_range(total)))
    def _():
        set_source(left, -asq[...])
        peak, exact = log_sum(right, left)
        out[...] = peak + jnp.log2(exact)


def source_weights(log_total, parts, growth, shift):
    rows = merged(parts[...])
    potential = FACTOR * (jnp.log2(growth[...]) - log_total - rows)
    log_weight = potential + shift[...]
    top = jnp.max(log_weight)
    return potential, jnp.exp2(log_weight - top), top


def weighted(lines, kernel):
    return jnp.dot(lines, kernel[...], preferred_element_type=f32)


def over_first(weight, kernel):
    return jnp.sum(weighted(rows_of(split3(weight), 16), kernel)[:3], axis=0, keepdims=True)


def columns(log_total, parts, growth, scores, shift, kernel, left0, right0, asq, bsq, out, sT, left, right):
    sT[...] = jnp.transpose(scores[...])
    potential, weight, top = source_weights(log_total, parts, growth, shift)
    total = over_first(weight, kernel)
    send_copies(out, top + jnp.log2(total))

    @pl.when(jnp.logical_not(in_range(total, weight)))
    def _():
        left[...] = left0[...]
        right[...] = right0[...]
        set_source(left, potential - asq[...])
        peak, exact = log_sum(left, right)
        send_copies(out, peak + jnp.log2(exact))


def rows(log_total, parts, shift, across, left0, right0, asq, bsq, out, left, right):
    potential = FACTOR * (-log_total - merged(parts[...]))
    top = jnp.max(potential)
    weight = jnp.exp2(potential - top)
    total = over_first(weight, across)
    out[...] = shift[...] + top + jnp.log2(total)

    @pl.when(jnp.logical_not(in_range(total, weight)))
    def _():
        left[...] = left0[...]
        right[...] = right0[...]
        set_source(left, -asq[...])
        set_target(right, potential - bsq[...])
        peak, exact = log_sum(right, left)
        out[...] = peak + jnp.log2(exact)


def pair(own, other, out):
    peak = jnp.maximum(own[...], other[...])
    total = jnp.exp2(own[...] - peak) + jnp.exp2(other[...] - peak)
    send_copies(out, peak + jnp.log2(total))


def put_blocks(out, carried, logs):
    count, lanes = out.shape[0], out.shape[2]
    progs = carried.shape[0]
    lines = jnp.concatenate([logs[:, d * lanes : (d + 1) * lanes] for d in range(count)], axis=0)
    for d in range(count):
        out[d, :progs, :] = carried[:, d * lanes : (d + 1) * lanes]
        out[d, progs:, :] = lines


def carry(log_total, parts, growth, shift, kernel, sT, left0, right0, asq, fout, out, left, right):
    potential, weight, top = source_weights(log_total, parts, growth, shift)
    fout[...] = potential * UNIT
    progs = sT.shape[0]
    scaled = sT[...].astype(f32) * weight
    high = scaled.astype(bf16)
    low = (scaled - high.astype(f32)).astype(bf16)
    sums = weighted(jnp.concatenate([high, low, rows_of(split3(weight), 16)], axis=0), kernel)
    total = jnp.sum(sums[2 * progs : 2 * progs + 3], axis=0, keepdims=True)
    put_blocks(out, (sums[:progs] + sums[progs : 2 * progs]) * (1.0 / total), top + jnp.log2(total))

    @pl.when(jnp.logical_not(in_range(total, weight)))
    def _():
        left[...] = left0[...]
        right[...] = right0[...]
        set_source(left, potential - asq[...])
        peak, exact = log_sum(left, right)

        def step(k, sums):
            plan = jnp.exp2(logits(tile_of(left, k), right[...]) - peak).astype(bf16)
            return sums + jnp.dot(tile_of(sT, k), plan, preferred_element_type=f32)

        start = jnp.zeros((progs, right.shape[1]), f32)
        sums = lax.fori_loop(0, left.shape[1] // TILE, step, start)
        put_blocks(out, sums / exact, peak + jnp.log2(exact))


def finish(log_total, parts, g, out):
    count, lanes = parts.shape[0], parts.shape[2]
    progs = parts.shape[1] - count
    g[...] = FACTOR * (-log_total - merged(parts[:, progs:, :])) * UNIT
    me = place_in_skewed(count)
    logs = [parts[d, pl.ds(progs + me, 1), :] for d in range(count)]
    peak = functools.reduce(jnp.maximum, logs)
    weights = [jnp.exp2(line - peak) for line in logs]
    total = sum(weights)
    carried = jnp.zeros((progs, lanes), f32)
    for d in range(count):
        carried = carried + (weights[d] / total) * parts[d, :progs, :]
    out[...] = jnp.broadcast_to(jnp.transpose(carried)[None], out.shape)


VMEM = pl.BlockSpec(memory_space=pltpu.VMEM)


def call(kernel, outs, specs, scratch=(), flops=10**7, name=None):
    return pl.pallas_call(
        kernel,
        out_shape=outs,
        in_specs=specs,
        scratch_shapes=list(scratch),
        compiler_params=pltpu.CompilerParams(vmem_limit_bytes=24 << 20),
        cost_estimate=pl.CostEstimate(flops=flops, bytes_accessed=1 << 20, transcendentals=0),
        name=name,
    )


def exchanged(x, axis, groups=None):
    return lax.all_to_all(x, axis, 0, 0, tiled=True, axis_index_groups=groups)


def rows_exchanged(line, targets):
    other = lax.ppermute(line, "tgt", [(k, k ^ 1) for k in range(targets)])
    copies = jax.ShapeDtypeStruct((targets // 2, *line.shape), f32)
    merged_line = call(pair, copies, [VMEM] * 2, name="pair")(line, other)
    chips = [[2 * ((z // 2 if z % 2 == 0 else targets // 2 - 1 - z // 2)) + core for z in range(targets // 2)] for core in range(2)]
    return exchanged(merged_line, "tgt", chips)


def skewed(sources):
    side = math.isqrt(sources)
    return [[(p // side) * side + (p + p // side) % side for p in range(sources)]]


def place_in_skewed(sources):
    side = math.isqrt(sources)
    me = lax.axis_index("src")
    y, x = me // side, me % side
    return y * side + (x - y + side) % side


def shards(pcs_source, pcs_target, growth, scores):
    count, size = pcs_source.shape
    progs = scores.shape[1]
    sources, targets = lax.axis_size("src"), lax.axis_size("tgt")
    own = size // sources
    log_sources = math.log2(size * sources)
    log_targets = math.log2(pcs_target.shape[1] * targets)
    scale = math.log2(math.e) / (EPSILON * count)
    shape = jax.ShapeDtypeStruct
    line = shape((1, size), f32)
    square = shape((size, size), bf16)
    operand = shape((DEPTH, size), bf16)
    operands = [pltpu.VMEM((DEPTH, size), bf16), pltpu.VMEM((DEPTH, size), bf16)]
    to_sources = shape((sources, 1, size), f32)

    pad = jnp.zeros((32 - count, size), bf16)
    local, left, right, asq, bsq, shift, kernel, across = call(
        functools.partial(first_rows, scale),
        (line, operand, operand, line, line, line, square, square),
        [VMEM],
        [pltpu.VMEM((size, DEPTH), bf16)],
        flops=4 * 10**9,
        name="first_rows",
    )(jnp.concatenate([pcs_source, pad, pcs_target, pad]))
    growth = growth.reshape(1, size)
    parts = rows_exchanged(local, targets)
    for _ in range(ITERS - 1):
        local, sT = call(
            functools.partial(columns, log_sources),
            (to_sources, shape((progs, size), bf16)),
            [VMEM] * 9,
            operands,
            name="columns",
        )(parts, growth, scores, shift, kernel, left, right, asq, bsq)
        parts = exchanged(local, "src", skewed(sources))
        local = call(functools.partial(rows, log_targets), line, [VMEM] * 7, operands, name="rows")(
            parts, shift, across, left, right, asq, bsq
        )
        parts = rows_exchanged(local, targets)
    potential, blocks = call(
        functools.partial(carry, log_sources),
        (line, shape((sources, progs + sources, own), f32)),
        [VMEM] * 8,
        operands,
        name="carry",
    )(parts, growth, shift, kernel, sT, left, right, asq)
    blocks = exchanged(blocks, "src", skewed(sources))
    g, result = call(
        functools.partial(finish, log_targets),
        (shape((sources, own), f32), shape((sources, own, progs), f32)),
        [VMEM],
        name="finish",
    )(blocks)
    transported = exchanged(result, "src", skewed(sources))
    return potential.reshape(size), g.reshape(size), transported.reshape(size, progs)


def solution(mesh):
    in_specs = (P(None, "src"), P(None, "tgt"), P("src"), P("src", None))
    out_specs = (P("src"), P("tgt"), P("tgt", None))
    return jax.shard_map(shards, mesh=mesh, in_specs=in_specs, out_specs=out_specs, check_vma=False)
```
